32 devices in a mesh: groups: 2 (over x), gx: 16 (over z, y, core).
Axes of the slice: x: 2, y: 2, z: 4, core: 2. Of those that a mesh axis runs over, the one named last changes fastest.
Arguments:
- features: bfloat16 [64, 16, 64, 128], P(('groups', 'gx')), parts along dimension 0, may hold values from -6 to 6
- cotangent: bfloat16 [64, 16, 64, 128], P(('groups', 'gx')), parts along dimension 0, may hold values from -6 to 6
- wall_flags: int32 [64, 16, 128], P(('groups', 'gx')), parts along dimension 0, may hold values 0 or 1
- mode_counts: int32 [64], replicated, may hold values from 1 to 16, as said below
- offsets: int32 [6, 3], replicated, may hold values from -2 to 2, as said below
- point_weight: bfloat16 [64, 64], replicated, may hold values from -0.75 to 0.75
- kernel_weight: bfloat16 [6, 64, 64], replicated, may hold values from -0.3125 to 0.3125
- lap_weight: bfloat16 [64, 64], replicated, may hold values from -0.125 to 0.125
- spec_weight: bfloat16 [16, 64, 64], replicated, may hold values from -1 to 1
- bias: float32 [64], replicated, may hold values from -3 to 3
Outputs:
- input_grad: bfloat16 [64, 16, 64, 128], P(('groups', 'gx')), parts along dimension 0
- kernel_grad: float32 [12, 64, 64], P('groups'), parts along dimension 0
The draws below stay inside these ranges and needn't reach their ends.
There are 2 independent parts, one for each index of `groups`. The reference program is written for one: setup_inputs(seed, part) draws one part's arguments, and reference() takes and returns one part's arrays. A program takes and returns all parts, laid end to end along the dimension named above; an argument that names none is the same for every part. Nothing has to cross between parts.
Inputs may be any that keep to these rules, and one draw needn't show every extreme that they name: Column 0 holds x offsets in -1..1 and both -1 and 1 occur; columns 1 and 2 hold y and z offsets in -2..2, and -2 and 2 occur in each of them. `mode_counts`: some channel keeps 16 modes and some channel keeps 1.
All inputs are finite; a program needn't handle non-finite values. No bound on the sum of `wall_flags` on one device may be relied on, other than what follows from the above.
Results may differ from the reference program's by a relative error of at most 0.0066.
Values may be sent and summed in bfloat16 or wider, within the bound.
A program may use at most 256 MiB of HBM per device.

```python
import math
from functools import partial
import jax
import jax.numpy as jnp
from jax import lax

C = 64
MX = 16
S = 6
RAD = 2
NZ = 128
NX = 32
NY = 16


def draw_offsets(key, part):
    key_along, key_across, key_depth, key_order = jax.random.split(key, 4)
    row_index = jnp.arange(S, dtype=jnp.int32)
    along_x = jax.random.randint(key_along, (S,), -1, 2, dtype=jnp.int32)
    along_y = jax.random.randint(key_across, (S,), -RAD, RAD + 1, dtype=jnp.int32)
    along_z = jax.random.randint(key_depth, (S,), -RAD, RAD + 1, dtype=jnp.int32)
    along_x = jnp.where(row_index == 0, 1, jnp.where(row_index == 1, -1, along_x))
    along_y = jnp.where(row_index == 2, RAD, jnp.where(row_index == 3, -RAD, along_y))
    along_z = jnp.where(row_index == 0, RAD, jnp.where(row_index == 1, -RAD, along_z))
    reorder = jax.random.permutation(key_order, S)
    return jnp.stack([along_x, along_y, along_z], axis=1)[reorder].astype(jnp.int32)


def draw_mode_counts(key, part):
    key_counts, key_first, key_second = jax.random.split(key, 3)
    counts = jax.random.randint(key_counts, (C,), 1, MX + 1, dtype=jnp.int32)
    first_row = jax.random.randint(key_first, (), 0, C, dtype=jnp.int32)
    second = (first_row + jax.random.randint(key_second, (), 1, C, dtype=jnp.int32)) % C
    row_index = jnp.arange(C, dtype=jnp.int32)
    counts = jnp.where(row_index == first_row, MX, counts)
    return jnp.where(row_index == second, 1, counts).astype(jnp.int32)


def place_ends(entries, stream_key, least, largest):
    shape = entries.shape
    place = [jax.random.randint(jax.random.fold_in(stream_key, axis), (), 0, shape[axis]) for axis in range(len(shape))]
    entries = entries.at[tuple(place)].set(least)
    longest = shape.index(max(shape))
    place[longest] = (place[longest] + 1) % shape[longest]
    return entries.at[tuple(place)].set(largest)


def shard_levels(key, shape, pieces, smallest, high):
    gain = 1.0
    for dim, shards_of in pieces:
        draws = jax.random.uniform(jax.random.fold_in(jax.random.fold_in(key, 6), dim), (shards_of,), jnp.float32, smallest / len(pieces), high / len(pieces))
        gain = gain * jnp.repeat(jnp.exp(draws), shape[dim] // shards_of).reshape((-1,) + (1,) * (len(shape) - 1 - dim))
    return gain


def noise(stream_key, extent, deviation, most, cuts=(), kind=jnp.bfloat16):
    values = deviation * jax.random.normal(stream_key, extent, jnp.float32)
    if cuts:
        values = values * shard_levels(stream_key, extent, cuts, -0.22, 0.18)
    return jnp.clip(values, -most, most).astype(kind)


def setup_inputs(seed: int = 0, part: int = 0) -> dict:
    key_of = jax.random.split(jax.random.key(seed), 11)
    part_splits = jax.random.split(jax.random.fold_in(key_of[10], part), 11)
    features = noise(part_splits[0], (NX, NY, C, NZ), 1.0, 6.0, ((0, 16),))
    cotangent = noise(part_splits[1], (NX, NY, C, NZ), 1.0, 6.0, ((0, 16),))
    wall_flags = place_ends((jax.random.randint(part_splits[2], (NX, NY, NZ), 0, 8) < 1).astype(jnp.int32), jax.random.fold_in(part_splits[2], 1), 0, 1)
    mode_counts = draw_mode_counts(jax.random.fold_in(key_of[10], 71), part)
    offsets = draw_offsets(jax.random.fold_in(key_of[10], 71), part)
    point_weight = noise(key_of[5], (C, C), C ** -0.5, 0.75)
    kernel_weight = noise(key_of[6], (S, C, C), (S * C) ** -0.5, 0.3125)
    lap_weight = noise(key_of[7], (C, C), (42 * C) ** -0.5, 0.125)
    spec_weight = noise(key_of[8], (MX, C, C), (max(1, MX * C // NX)) ** -0.5, 1.0)
    bias = noise(key_of[9], (C,), 0.5, 3.0, (), jnp.float32)
    return {"features": features, "cotangent": cotangent, "wall_flags": wall_flags, "mode_counts": mode_counts, "offsets": offsets, "point_weight": point_weight, "kernel_weight": kernel_weight, "lap_weight": lap_weight, "spec_weight": spec_weight, "bias": bias}


def basis_table(mode_total, length):
    mode_index = jnp.arange(mode_total, dtype=jnp.float32)[:, None]
    cell_index = jnp.arange(length, dtype=jnp.float32)[None, :]
    phase_angle = math.pi / (2.0 * length) * mode_index * (2.0 * cell_index + 1.0)
    amplitude = jnp.where(mode_index == 0.0, math.sqrt(1.0 / length), math.sqrt(2.0 / length))
    return (amplitude * jnp.cos(phase_angle)).astype(jnp.bfloat16)

def spectral(values, spec_weight, kept_modes, basis, adjoint):
    wide_basis = basis.astype(jnp.float32)
    coefficients = jnp.einsum('kx,xycz->kycz', wide_basis, values.astype(jnp.float32)).astype(jnp.bfloat16)
    weights = spec_weight.astype(jnp.float32)
    if adjoint:
        masked = coefficients.astype(jnp.float32) * kept_modes[:, None, :, None]
        mixed_modes = jnp.einsum('koc,kyoz->kycz', weights, masked).astype(jnp.bfloat16)
    else:
        mixed_modes = jnp.einsum('koc,kycz->kyoz', weights, coefficients.astype(jnp.float32))
        mixed_modes = (mixed_modes * kept_modes[:, None, :, None]).astype(jnp.bfloat16)
    return jnp.einsum('kx,kyoz->xyoz', wide_basis, mixed_modes.astype(jnp.float32)).astype(jnp.bfloat16)

def laplace(values):
    padded = jnp.pad(values.astype(jnp.float32), ((1, 1), (1, 1), (0, 0), (1, 1)))
    centre_cells = padded[1:-1, 1:-1, :, 1:-1]
    neighbours = padded[2:, 1:-1, :, 1:-1] + padded[:-2, 1:-1, :, 1:-1]
    neighbours = neighbours + padded[1:-1, 2:, :, 1:-1] + padded[1:-1, :-2, :, 1:-1]
    neighbours = neighbours + padded[1:-1, 1:-1, :, 2:] + padded[1:-1, 1:-1, :, :-2]
    return (neighbours - 6.0 * centre_cells).astype(jnp.bfloat16)

def shifted(values, offset, direction):
    padded = jnp.pad(values, ((1, 1), (RAD, RAD), (0, 0), (RAD, RAD)))
    starts = ((1 + direction * offset[0]).astype(jnp.int32), (RAD + direction * offset[1]).astype(jnp.int32), jnp.int32(0), (RAD + direction * offset[2]).astype(jnp.int32))
    return lax.dynamic_slice(padded, starts, values.shape)

def mix_forward(weight, values):
    return jnp.einsum('oc,xycz->xyoz', weight.astype(jnp.float32), values.astype(jnp.float32))

def mix_back(weight, values):
    return jnp.einsum('oc,xyoz->xycz', weight.astype(jnp.float32), values.astype(jnp.float32))

def reference(features, cotangent, wall_flags, mode_counts, offsets, point_weight, kernel_weight, lap_weight, spec_weight, bias):
    basis = basis_table(MX, NX)
    kept_modes = (jnp.arange(MX, dtype=jnp.int32)[:, None] < mode_counts[None, :]).astype(jnp.float32)
    fluid_mask = (1 - wall_flags).astype(jnp.float32)[:, :, None, :]
    spectral_part = spectral(features, spec_weight, kept_modes, basis, False)
    lap_field = laplace(features)
    preact = mix_forward(point_weight, features) + mix_forward(lap_weight, lap_field)
    preact = preact + spectral_part.astype(jnp.float32) + bias[None, None, :, None]
    for tile in range(S):
        preact = preact + mix_forward(kernel_weight[tile], shifted(features, offsets[tile], 1))
    _, pullback = jax.vjp(partial(jax.nn.gelu, approximate=True), preact)
    weighted = (pullback(cotangent.astype(jnp.float32))[0] * fluid_mask).astype(jnp.bfloat16)
    spec_grad = spectral(weighted, spec_weight, kept_modes, basis, True)
    lap_grad = laplace(weighted)
    input_grad = mix_back(point_weight, weighted) + mix_back(lap_weight, lap_grad) + spec_grad.astype(jnp.float32)
    scaling = float(NX * NY * NZ) ** (-0.5)
    tile_grads = []
    wide_weighted = weighted.astype(jnp.float32)
    for tile in range(S):
        input_grad = input_grad + mix_back(kernel_weight[tile], shifted(weighted, offsets[tile], -1))
        moved = shifted(features, offsets[tile], 1).astype(jnp.float32)
        tile_grads.append(jnp.einsum('xyoz,xycz->oc', wide_weighted, moved) * scaling)
    kernel_grad = jnp.stack(tile_grads, axis=0)
    return (input_grad.astype(jnp.bfloat16), kernel_grad)
```

```python
from functools import partial
import math

import jax
import jax.numpy as jnp
from jax import lax
from jax.sharding import PartitionSpec as P

RAD = 2


def with_halo(cells, sides, width):
    for axis, dim in sides:
        count = lax.axis_size(axis)
        ends = count - 1
        head = lax.slice_in_dim(cells, 0, width, axis=dim)
        tail = lax.slice_in_dim(cells, cells.shape[dim] - width, cells.shape[dim], axis=dim)
        cells = jnp.concatenate(
            [
                lax.ppermute(tail, axis, [(i, (i + 1) % count) for i in range(ends)]),
                cells,
                lax.ppermute(head, axis, [((i + 1) % count, i) for i in range(ends)]),
            ],
            axis=dim,
        )
    return cells


def basis_table(mode_total, length):
    mode_index = jnp.arange(mode_total, dtype=jnp.float32)[:, None]
    cell_index = jnp.arange(length, dtype=jnp.float32)[None, :]
    phase_angle = math.pi / (2.0 * length) * mode_index * (2.0 * cell_index + 1.0)
    amplitude = jnp.where(mode_index == 0.0, math.sqrt(1.0 / length), math.sqrt(2.0 / length))
    return (amplitude * jnp.cos(phase_angle)).astype(jnp.bfloat16)


def pencil_work(pencil, spec_weight, kept_modes, adjoint):
    basis = basis_table(spec_weight.shape[0], pencil.shape[0])
    coefficients = jnp.einsum(
        "kx,xycz->kycz", basis, pencil, preferred_element_type=jnp.float32
    ).astype(jnp.bfloat16)
    if adjoint:
        masked = coefficients * kept_modes[:, None, :, None].astype(jnp.bfloat16)
        mixed_modes = jnp.einsum(
            "koc,kyoz->kycz", spec_weight, masked, preferred_element_type=jnp.float32
        ).astype(jnp.bfloat16)
    else:
        mixed_modes = jnp.einsum(
            "koc,kycz->kyoz", spec_weight, coefficients, preferred_element_type=jnp.float32
        )
        mixed_modes = (mixed_modes * kept_modes[:, None, :, None]).astype(jnp.bfloat16)
    return jnp.einsum(
        "kx,kyoz->xyoz", basis, mixed_modes, preferred_element_type=jnp.float32
    ).astype(jnp.bfloat16)


def spectral(slab, spec_weight, kept_modes, adjoint):
    result = pencil_work(
        lax.all_to_all(slab, "gx", split_axis=1, concat_axis=0, tiled=True),
        spec_weight,
        kept_modes,
        adjoint,
    )
    return lax.all_to_all(result, "gx", split_axis=0, concat_axis=1, tiled=True)


def laplace_ext(extended):
    padded = jnp.pad(extended, ((0, 0), (1, 1), (0, 0), (1, 1))).astype(jnp.float32)
    centre_cells = padded[1:-1, 1:-1, :, 1:-1]
    neighbours = padded[2:, 1:-1, :, 1:-1] + padded[:-2, 1:-1, :, 1:-1]
    neighbours = neighbours + padded[1:-1, 2:, :, 1:-1] + padded[1:-1, :-2, :, 1:-1]
    neighbours = neighbours + padded[1:-1, 1:-1, :, 2:] + padded[1:-1, 1:-1, :, :-2]
    return (neighbours - 6.0 * centre_cells).astype(jnp.bfloat16)


def pad_sides(extended):
    return jnp.pad(extended, ((0, 0), (RAD, RAD), (0, 0), (RAD, RAD)))


def window_of(padded, offset, direction, slab_shape):
    starts = (
        1 + direction * offset[0],
        RAD + direction * offset[1],
        0,
        RAD + direction * offset[2],
    )
    return lax.dynamic_slice(padded, starts, slab_shape)


def gelu_slope(preact, upstream):
    _, pullback = jax.vjp(partial(jax.nn.gelu, approximate=True), preact)
    return pullback(upstream)[0]


def sum_over_gx(terms):
    count = lax.axis_size("gx")
    if terms.size % count:
        return lax.psum(terms, "gx")
    pieces = lax.all_to_all(terms.reshape(count, -1), "gx", split_axis=0, concat_axis=0, tiled=True)
    mine = jnp.sum(pieces, axis=0)
    copies = jnp.broadcast_to(mine[None, :], pieces.shape)
    gathered = lax.all_to_all(copies, "gx", split_axis=0, concat_axis=0, tiled=True)
    return gathered.reshape(terms.shape)


def per_device(
    features,
    cotangent,
    wall_flags,
    mode_counts,
    offsets,
    point_weight,
    kernel_weight,
    lap_weight,
    spec_weight,
    bias,
):
    mode_total = spec_weight.shape[0]
    tile_total = kernel_weight.shape[0]
    kept_modes = (jnp.arange(mode_total, dtype=jnp.int32)[:, None] < mode_counts[None, :]).astype(
        jnp.float32
    )
    fluid_mask = (1 - wall_flags).astype(jnp.float32)[:, :, None, :]
    extended = with_halo(features, (("gx", 0),), 1)
    padded_field = pad_sides(extended)
    local_part = jnp.einsum(
        "oc,xycz->xyoz", point_weight, features, preferred_element_type=jnp.float32
    )
    local_part = local_part + jnp.einsum(
        "oc,xycz->xyoz", lap_weight, laplace_ext(extended), preferred_element_type=jnp.float32
    )
    for tile in range(tile_total):
        moved = window_of(padded_field, offsets[tile], 1, features.shape)
        local_part = local_part + jnp.einsum(
            "oc,xycz->xyoz", kernel_weight[tile], moved, preferred_element_type=jnp.float32
        )
    local_part = local_part + bias[:, None]
    spectral_part = spectral(features, spec_weight, kept_modes, False)
    preact = local_part + spectral_part.astype(jnp.float32)
    weighted = (gelu_slope(preact, cotangent.astype(jnp.float32)) * fluid_mask).astype(jnp.bfloat16)
    spec_grad = spectral(weighted, spec_weight, kept_modes, True)
    ext_grad = with_halo(weighted, (("gx", 0),), 1)
    padded_grad = pad_sides(ext_grad)
    input_grad = jnp.einsum(
        "oc,xyoz->xycz", point_weight, weighted, preferred_element_type=jnp.float32
    )
    input_grad = input_grad + jnp.einsum(
        "oc,xyoz->xycz", lap_weight, laplace_ext(ext_grad), preferred_element_type=jnp.float32
    )
    input_grad = input_grad + spec_grad.astype(jnp.float32)
    tile_grads = []
    for tile in range(tile_total):
        back_moved = window_of(padded_grad, offsets[tile], -1, weighted.shape)
        input_grad = input_grad + jnp.einsum(
            "oc,xyoz->xycz", kernel_weight[tile], back_moved, preferred_element_type=jnp.float32
        )
        tile_grads.append(
            jnp.einsum("xyoz,xycz->oc", back_moved, features, preferred_element_type=jnp.float32)
        )
    local_grad = jnp.stack(tile_grads, axis=0)
    scaling = float(
        lax.axis_size("gx") * features.shape[0] * features.shape[1] * features.shape[3]
    ) ** (-0.5)
    summed = sum_over_gx(local_grad)
    return (input_grad.astype(jnp.bfloat16), summed * scaling)


def solution(mesh):
    return jax.shard_map(
        per_device,
        mesh=mesh,
        in_specs=(
            P(("groups", "gx"), None, None, None),
            P(("groups", "gx"), None, None, None),
            P(("groups", "gx"), None, None),
            P(),
            P(),
            P(),
            P(),
            P(),
            P(),
            P(),
        ),
        out_specs=(P(("groups", "gx"), None, None, None), P("groups", None, None)),
        check_vma=False,
    )
```

```python
import functools
from functools import partial
import math

import jax
import jax.numpy as jnp
from jax import lax
from jax.experimental import pallas as pl
from jax.experimental.pallas import tpu as pltpu
from jax.sharding import PartitionSpec as P

RAD = 2
MESH = pl.DeviceIdType.MESH


def with_halo(cells, sides, width):
    for axis, dim in sides:
        count = lax.axis_size(axis)
        ends = count - 1
        head = lax.slice_in_dim(cells, 0, width, axis=dim)
        tail = lax.slice_in_dim(cells, cells.shape[dim] - width, cells.shape[dim], axis=dim)
        cells = jnp.concatenate(
            [
                lax.ppermute(tail, axis, [(i, (i + 1) % count) for i in range(ends)]),
                cells,
                lax.ppermute(head, axis, [((i + 1) % count, i) for i in range(ends)]),
            ],
            axis=dim,
        )
    return cells


def basis_table(mode_total, length):
    mode_index = jnp.arange(mode_total, dtype=jnp.float32)[:, None]
    cell_index = jnp.arange(length, dtype=jnp.float32)[None, :]
    phase_angle = math.pi / (2.0 * length) * mode_index * (2.0 * cell_index + 1.0)
    amplitude = jnp.where(mode_index == 0.0, math.sqrt(1.0 / length), math.sqrt(2.0 / length))
    return (amplitude * jnp.cos(phase_angle)).astype(jnp.bfloat16)


def pencil_work(pencil, spec_weight, kept_modes, adjoint):
    basis = basis_table(spec_weight.shape[0], pencil.shape[0])
    coefficients = jnp.einsum(
        "kx,xycz->kycz", basis, pencil, preferred_element_type=jnp.float32
    ).astype(jnp.bfloat16)
    if adjoint:
        masked = coefficients * kept_modes[:, None, :, None].astype(jnp.bfloat16)
        mixed_modes = jnp.einsum(
            "koc,kyoz->kycz", spec_weight, masked, preferred_element_type=jnp.float32
        ).astype(jnp.bfloat16)
    else:
        mixed_modes = jnp.einsum(
            "koc,kycz->kyoz", spec_weight, coefficients, preferred_element_type=jnp.float32
        )
        mixed_modes = (mixed_modes * kept_modes[:, None, :, None]).astype(jnp.bfloat16)
    return jnp.einsum(
        "kx,kyoz->xyoz", basis, mixed_modes, preferred_element_type=jnp.float32
    ).astype(jnp.bfloat16)


def spectral(slab, spec_weight, kept_modes, adjoint):
    result = pencil_work(
        lax.all_to_all(slab, "gx", split_axis=1, concat_axis=0, tiled=True),
        spec_weight,
        kept_modes,
        adjoint,
    )
    return lax.all_to_all(result, "gx", split_axis=0, concat_axis=1, tiled=True)


def laplace_ext(extended):
    padded = jnp.pad(extended, ((0, 0), (1, 1), (0, 0), (1, 1))).astype(jnp.float32)
    centre_cells = padded[1:-1, 1:-1, :, 1:-1]
    neighbours = padded[2:, 1:-1, :, 1:-1] + padded[:-2, 1:-1, :, 1:-1]
    neighbours = neighbours + padded[1:-1, 2:, :, 1:-1] + padded[1:-1, :-2, :, 1:-1]
    neighbours = neighbours + padded[1:-1, 1:-1, :, 2:] + padded[1:-1, 1:-1, :, :-2]
    return (neighbours - 6.0 * centre_cells).astype(jnp.bfloat16)


def pad_sides(extended):
    return jnp.pad(extended, ((0, 0), (RAD, RAD), (0, 0), (RAD, RAD)))


def window_of(padded, offset, direction, slab_shape):
    starts = (
        1 + direction * offset[0],
        RAD + direction * offset[1],
        0,
        RAD + direction * offset[2],
    )
    return lax.dynamic_slice(padded, starts, slab_shape)


def gelu_slope(preact, upstream):
    _, pullback = jax.vjp(partial(jax.nn.gelu, approximate=True), preact)
    return pullback(upstream)[0]


def sum_over_gx(terms):
    count = lax.axis_size("gx")
    if terms.size % count:
        return lax.psum(terms, "gx")
    pieces = lax.all_to_all(terms.reshape(count, -1), "gx", split_axis=0, concat_axis=0, tiled=True)
    mine = jnp.sum(pieces, axis=0)
    copies = jnp.broadcast_to(mine[None, :], pieces.shape)
    gathered = lax.all_to_all(copies, "gx", split_axis=0, concat_axis=0, tiled=True)
    return gathered.reshape(terms.shape)


def per_device(
    features,
    cotangent,
    wall_flags,
    mode_counts,
    offsets,
    point_weight,
    kernel_weight,
    lap_weight,
    spec_weight,
    bias,
):
    mode_total = spec_weight.shape[0]
    tile_total = kernel_weight.shape[0]
    kept_modes = (jnp.arange(mode_total, dtype=jnp.int32)[:, None] < mode_counts[None, :]).astype(
        jnp.float32
    )
    fluid_mask = (1 - wall_flags).astype(jnp.float32)[:, :, None, :]
    extended = with_halo(features, (("gx", 0),), 1)
    padded_field = pad_sides(extended)
    local_part = jnp.einsum(
        "oc,xycz->xyoz", point_weight, features, preferred_element_type=jnp.float32
    )
    local_part = local_part + jnp.einsum(
        "oc,xycz->xyoz", lap_weight, laplace_ext(extended), preferred_element_type=jnp.float32
    )
    for tile in range(tile_total):
        moved = window_of(padded_field, offsets[tile], 1, features.shape)
        local_part = local_part + jnp.einsum(
            "oc,xycz->xyoz", kernel_weight[tile], moved, preferred_element_type=jnp.float32
        )
    local_part = local_part + bias[:, None]
    spectral_part = spectral(features, spec_weight, kept_modes, False)
    preact = local_part + spectral_part.astype(jnp.float32)
    weighted = (gelu_slope(preact, cotangent.astype(jnp.float32)) * fluid_mask).astype(jnp.bfloat16)
    spec_grad = spectral(weighted, spec_weight, kept_modes, True)
    ext_grad = with_halo(weighted, (("gx", 0),), 1)
    padded_grad = pad_sides(ext_grad)
    input_grad = jnp.einsum(
        "oc,xyoz->xycz", point_weight, weighted, preferred_element_type=jnp.float32
    )
    input_grad = input_grad + jnp.einsum(
        "oc,xyoz->xycz", lap_weight, laplace_ext(ext_grad), preferred_element_type=jnp.float32
    )
    input_grad = input_grad + spec_grad.astype(jnp.float32)
    tile_grads = []
    for tile in range(tile_total):
        back_moved = window_of(padded_grad, offsets[tile], -1, weighted.shape)
        input_grad = input_grad + jnp.einsum(
            "oc,xyoz->xycz", kernel_weight[tile], back_moved, preferred_element_type=jnp.float32
        )
        tile_grads.append(
            jnp.einsum("xyoz,xycz->oc", back_moved, features, preferred_element_type=jnp.float32)
        )
    local_grad = jnp.stack(tile_grads, axis=0)
    scaling = float(
        lax.axis_size("gx") * features.shape[0] * features.shape[1] * features.shape[3]
    ) ** (-0.5)
    summed = sum_over_gx(local_grad)
    return (input_grad.astype(jnp.bfloat16), summed * scaling)


def fused_kernel(
    count,
    feat,
    cot,
    wall,
    offs,
    basis,
    wf,
    wb,
    wm,
    wmt,
    bias,
    out,
    kout,
    zs,
    cat,
    local,
    acc,
    vh,
    pen1,
    pen2,
    stage1,
    stage2,
    spec1,
    spec2,
    wgt,
    halo1,
    halo2,
    kacc,
    kpart,
    ksum,
    kall,
    send,
    recv,
    hsend,
    hrecv,
):
    me = lax.axis_index("gx")
    grp = lax.axis_index("groups")
    xl, ny, ch, nz = feat.shape
    modes = wm.shape[0]
    tiles = offs.shape[0]
    f32, bf16 = jnp.float32, jnp.bfloat16

    def remote(src, dst, phase, d, peer):
        return pltpu.make_async_remote_copy(
            src_ref=src,
            dst_ref=dst,
            send_sem=send.at[phase, d],
            recv_sem=recv.at[phase, d],
            device_id=(grp, peer),
            device_id_type=MESH,
        )

    def ahead(d):
        return lax.rem(me + d, count)

    def behind(d):
        return lax.rem(me + count - d, count)

    def halo_copy(src, dst, slot, peer):
        return pltpu.make_async_remote_copy(
            src_ref=src,
            dst_ref=dst,
            send_sem=hsend.at[slot],
            recv_sem=hrecv.at[slot],
            device_id=(grp, peer),
            device_id_type=MESH,
        )

    def each(low, high, body):
        def step(i, carry):
            body(i)
            return carry

        lax.fori_loop(low, high, step, 0)

    barrier = pltpu.get_barrier_semaphore()
    each(
        1,
        count,
        lambda d: pl.semaphore_signal(
            barrier, inc=1, device_id=(grp, ahead(d)), device_id_type=MESH
        ),
    )
    pl.semaphore_wait(barrier, count - 1)

    def halo_start(low_plane, high_plane, halo, base):
        @pl.when(me > 0)
        def _():
            halo_copy(low_plane, halo.at[1], base, me - 1).start()

        @pl.when(me < count - 1)
        def _():
            halo_copy(high_plane, halo.at[0], base + 1, me + 1).start()

        @pl.when(me == 0)
        def _():
            halo[0] = jnp.zeros(halo.shape[1:], bf16)

        @pl.when(me == count - 1)
        def _():
            halo[1] = jnp.zeros(halo.shape[1:], bf16)

    def halo_wait(low_plane, high_plane, halo, base):
        @pl.when(me > 0)
        def _():
            halo_copy(low_plane, halo.at[1], base, me - 1).wait_send()
            halo_copy(high_plane, halo.at[0], base + 1, me - 1).wait_recv()

        @pl.when(me < count - 1)
        def _():
            halo_copy(high_plane, halo.at[0], base + 1, me + 1).wait_send()
            halo_copy(low_plane, halo.at[1], base, me + 1).wait_recv()

    lane = lax.broadcasted_iota(jnp.int32, (ch, nz), 1)

    def spread(load, place):
        def body(y):
            v = load(y)
            zs[RAD, place, y + RAD] = v
            wide = v.astype(f32)
            for dz in range(-RAD, RAD + 1):
                if dz:
                    moved = pltpu.roll(wide, (-dz) % nz, 1)
                    inside = lane < nz - dz if dz > 0 else lane >= -dz
                    zs[RAD + dz, place, y + RAD] = jnp.where(inside, moved, 0.0).astype(bf16)

        each(0, ny, body)

    def gather_rows(direction):
        def body(y):
            for x in range(xl):
                lanes = slice(x * nz, (x + 1) * nz)
                centre = zs[RAD, x + 1, y + RAD]
                cat[y, 0:ch, lanes] = centre
                total = zs[RAD, x + 2, y + RAD].astype(f32) + zs[RAD, x, y + RAD].astype(f32)
                total = total + zs[RAD, x + 1, y + RAD + 1].astype(f32)
                total = total + zs[RAD, x + 1, y + RAD - 1].astype(f32)
                total = total + zs[RAD + 1, x + 1, y + RAD].astype(f32)
                total = total + zs[RAD - 1, x + 1, y + RAD].astype(f32)
                cat[y, ch : 2 * ch, lanes] = (total - 6.0 * centre.astype(f32)).astype(bf16)
                for t in range(tiles):
                    moved = zs[
                        RAD + direction * offs[t, 2],
                        x + 1 + direction * offs[t, 0],
                        y + RAD + direction * offs[t, 1],
                    ]
                    cat[y, (2 + t) * ch : (3 + t) * ch, lanes] = moved

        each(0, ny, body)

    def mix(weights):
        def body(y):
            local[y] = jnp.dot(weights[...], cat[y], preferred_element_type=f32)

        each(0, ny, body)

    def gain(planes, src):
        wide = [p.astype(f32) for p in planes]
        for k in range(modes):
            total = acc[k]
            for j in range(xl):
                total = total + basis[k, src * xl + j] * wide[j]
            acc[k] = total

    def channel_mix(weights):
        for k in range(modes):
            u = acc[k].astype(bf16)
            v = jnp.dot(weights[k], u, preferred_element_type=f32)
            vh[k] = v.astype(bf16).astype(f32)

    def expand(stage, peer):
        for j in range(xl):
            total = basis[0, peer * xl + j] * vh[0]
            for k in range(1, modes):
                total = total + basis[k, peer * xl + j] * vh[k]
            stage[peer, j] = total.astype(bf16)

    each(1, count, lambda d: remote(feat.at[:, ahead(d)], pen1.at[me], 0, d, ahead(d)).start())
    low1, high1 = feat.at[0], feat.at[xl - 1]
    halo_start(low1, high1, halo1, 0)

    for edge in (0, RAD + ny):
        for dz in range(2 * RAD + 1):
            for x in range(xl + 2):
                zs[dz, x, edge : edge + RAD] = jnp.zeros((RAD, ch, nz), bf16)
    for x in range(xl):
        spread(lambda y: feat[x, y], x + 1)
    acc[...] = jnp.zeros(acc.shape, f32)
    gain([feat[j, me] for j in range(xl)], me)
    halo_wait(low1, high1, halo1, 0)
    spread(lambda y: halo1[0, y], 0)
    spread(lambda y: halo1[1, y], xl + 1)
    gather_rows(1)

    def take1(d):
        src = behind(d)
        remote(feat.at[:, src], pen1.at[src], 0, d, src).wait_recv()
        gain([pen1[src, j] for j in range(xl)], src)

    each(1, count, take1)
    channel_mix(wm)

    def give1(d):
        peer = ahead(d)
        expand(stage1, peer)
        remote(stage1.at[peer], spec1.at[me], 1, d, peer).start()

    each(1, count, give1)
    expand(stage1, me)
    mix(wf)
    root = math.sqrt(2.0 / math.pi)

    def slope(y, planes):
        for x in range(xl):
            v = local[y, :, x * nz : (x + 1) * nz] + planes[x].astype(f32) + bias[...]
            square = v * v
            t = jnp.tanh(root * (v + 0.044715 * (square * v)))
            g = 0.5 * (1.0 + t)
            g = g + (0.5 * v) * ((1.0 - t * t) * (root * (1.0 + (3.0 * 0.044715) * square)))
            fluid = (1 - wall[x, pl.ds(y, 1), :]).astype(f32)
            wgt[y, x] = ((cot[x, y].astype(f32) * g) * fluid).astype(bf16)

    slope(me, [stage1[me, j] for j in range(xl)])

    def turn(d):
        src = behind(d)
        remote(stage1.at[src], spec1.at[src], 1, d, src).wait_recv()
        slope(src, [spec1[src, j] for j in range(xl)])
        remote(wgt.at[src], pen2.at[me], 2, count - d, src).start()

    each(1, count, turn)

    low2, high2 = wgt.at[:, 0], wgt.at[:, xl - 1]
    halo_start(low2, high2, halo2, 2)
    for x in range(xl):
        spread(lambda y: wgt[y, x], x + 1)
    acc[...] = jnp.zeros(acc.shape, f32)
    gain([wgt[me, j] for j in range(xl)], me)
    halo_wait(low2, high2, halo2, 2)
    spread(lambda y: halo2[0, y], 0)
    spread(lambda y: halo2[1, y], xl + 1)
    gather_rows(-1)

    def take2(i):
        d = count - i
        src = behind(d)
        remote(wgt.at[src], pen2.at[src], 2, d, src).wait_recv()
        gain([pen2[src, j] for j in range(xl)], src)

    each(1, count, take2)
    channel_mix(wmt)

    def give2(d):
        peer = ahead(d)
        expand(stage2, peer)
        remote(stage2.at[peer], spec2.at[me], 3, d, peer).start()

    each(1, count, give2)
    expand(stage2, me)

    kacc[...] = jnp.zeros(kacc.shape, f32)

    def tile_grad(y):
        field = jnp.concatenate([feat[x, y] for x in range(xl)], axis=1)
        kacc[...] += lax.dot_general(
            cat[y, 2 * ch :, :], field, (((1,), (1,)), ((), ())), preferred_element_type=f32
        )

    each(0, ny, tile_grad)
    rows = kpart.shape[1]
    for p in range(count):
        kpart[p] = kacc[p * rows : (p + 1) * rows]
    each(1, count, lambda d: remote(kpart.at[ahead(d)], ksum.at[me], 4, d, ahead(d)).start())
    mix(wb)
    ksum[me] = kpart[me]
    each(1, count, lambda d: remote(kpart.at[0], ksum.at[behind(d)], 4, d, behind(d)).wait_recv())
    total = ksum[0]
    for p in range(1, count):
        total = total + ksum[p]
    kall[me] = total * (float(count * xl * ny * nz) ** -0.5)
    each(1, count, lambda d: remote(kall.at[me], kall.at[me], 5, d, ahead(d)).start())

    def finish(y, planes):
        for x in range(xl):
            total = local[y, :, x * nz : (x + 1) * nz] + planes[x].astype(f32)
            out[x, y] = total.astype(bf16)

    finish(me, [stage2[me, j] for j in range(xl)])

    def last(d):
        src = behind(d)
        remote(stage2.at[src], spec2.at[src], 3, d, src).wait_recv()
        finish(src, [spec2[src, j] for j in range(xl)])

    each(1, count, last)
    each(1, count, lambda d: remote(kall.at[me], kall.at[behind(d)], 5, d, behind(d)).wait_recv())
    kout[...] = kall[...]

    def drain(d):
        peer = ahead(d)
        remote(feat.at[:, peer], pen1.at[me], 0, d, peer).wait_send()
        remote(stage1.at[peer], spec1.at[me], 1, d, peer).wait_send()
        remote(wgt.at[peer], pen2.at[me], 2, d, peer).wait_send()
        remote(stage2.at[peer], spec2.at[me], 3, d, peer).wait_send()
        remote(kpart.at[peer], ksum.at[me], 4, d, peer).wait_send()
        remote(kall.at[me], kall.at[me], 5, d, peer).wait_send()

    each(1, count, drain)


def fits_kernel(count, features, kernel_weight):
    xl, ny, ch, nz = features.shape
    cells = xl * ny * ch * nz
    tile_rows = kernel_weight.shape[0] * ch
    if ny != count or nz % 128 or ch % 16 or tile_rows % (8 * count):
        return False
    return 80 * cells < 24 * 2**20


def fused_device(
    features,
    cotangent,
    wall_flags,
    mode_counts,
    offsets,
    point_weight,
    kernel_weight,
    lap_weight,
    spec_weight,
    bias,
):
    count = lax.axis_size("gx")
    if not fits_kernel(count, features, kernel_weight):
        return per_device(
            features,
            cotangent,
            wall_flags,
            mode_counts,
            offsets,
            point_weight,
            kernel_weight,
            lap_weight,
            spec_weight,
            bias,
        )
    xl, ny, ch, nz = features.shape
    modes, tiles = spec_weight.shape[0], kernel_weight.shape[0]
    kept = jnp.arange(modes, dtype=jnp.int32)[:, None] < mode_counts[None, :]
    masked = jnp.where(kept[:, :, None], spec_weight, jnp.zeros_like(spec_weight))
    stacked = jnp.concatenate([point_weight[None], lap_weight[None], kernel_weight], axis=0)
    forward = jnp.transpose(stacked, (1, 0, 2)).reshape(ch, (2 + tiles) * ch)
    backward = jnp.transpose(stacked, (2, 0, 1)).reshape(ch, (2 + tiles) * ch)
    rows = tiles * ch // count
    f32, bf16 = jnp.float32, jnp.bfloat16
    vmem = pl.BlockSpec(memory_space=pltpu.VMEM)
    smem = pl.BlockSpec(memory_space=pltpu.SMEM)
    field_grad, tile_grad = pl.pallas_call(
        functools.partial(fused_kernel, count),
        out_shape=(
            jax.ShapeDtypeStruct(features.shape, bf16),
            jax.ShapeDtypeStruct((count, rows, ch), f32),
        ),
        in_specs=[vmem, vmem, vmem, smem, smem, vmem, vmem, vmem, vmem, vmem],
        out_specs=(vmem, vmem),
        scratch_shapes=[
            pltpu.VMEM((2 * RAD + 1, xl + 2, ny + 2 * RAD, ch, nz), bf16),
            pltpu.VMEM((ny, (2 + tiles) * ch, xl * nz), bf16),
            pltpu.VMEM((ny, ch, xl * nz), f32),
            pltpu.VMEM((modes, ch, nz), f32),
            pltpu.VMEM((modes, ch, nz), f32),
            pltpu.VMEM((count, xl, ch, nz), bf16),
            pltpu.VMEM((count, xl, ch, nz), bf16),
            pltpu.VMEM((count, xl, ch, nz), bf16),
            pltpu.VMEM((count, xl, ch, nz), bf16),
            pltpu.VMEM((count, xl, ch, nz), bf16),
            pltpu.VMEM((count, xl, ch, nz), bf16),
            pltpu.VMEM((ny, xl, ch, nz), bf16),
            pltpu.VMEM((2, ny, ch, nz), bf16),
            pltpu.VMEM((2, ny, ch, nz), bf16),
            pltpu.VMEM((tiles * ch, ch), f32),
            pltpu.VMEM((count, rows, ch), f32),
            pltpu.VMEM((count, rows, ch), f32),
            pltpu.VMEM((count, rows, ch), f32),
            pltpu.SemaphoreType.DMA((6, count)),
            pltpu.SemaphoreType.DMA((6, count)),
            pltpu.SemaphoreType.DMA((4,)),
            pltpu.SemaphoreType.DMA((4,)),
        ],
        compiler_params=pltpu.CompilerParams(
            collective_id=0, has_side_effects=True, vmem_limit_bytes=48 * 2**20
        ),
    )(
        features,
        cotangent,
        wall_flags,
        offsets,
        basis_table(modes, count * xl).astype(f32),
        forward,
        backward,
        masked,
        jnp.swapaxes(masked, 1, 2),
        jnp.broadcast_to(bias[:, None], (ch, nz)),
    )
    return field_grad, tile_grad.reshape(kernel_weight.shape)


def solution(mesh):
    return jax.shard_map(
        fused_device,
        mesh=mesh,
        in_specs=(
            P(("groups", "gx"), None, None, None),
            P(("groups", "gx"), None, None, None),
            P(("groups", "gx"), None, None),
            P(),
            P(),
            P(),
            P(),
            P(),
            P(),
            P(),
        ),
        out_specs=(P(("groups", "gx"), None, None, None), P("groups", None, None)),
        check_vma=False,
    )
```

```python
import functools
from functools import partial
import math

import jax
import jax.numpy as jnp
from jax import lax
from jax.experimental import pallas as pl
from jax.experimental.pallas import tpu as pltpu
from jax.sharding import PartitionSpec as P

RAD = 2
MESH = pl.DeviceIdType.MESH


def with_halo(cells, sides, width):
    for axis, dim in sides:
        count = lax.axis_size(axis)
        ends = count - 1
        head = lax.slice_in_dim(cells, 0, width, axis=dim)
        tail = lax.slice_in_dim(cells, cells.shape[dim] - width, cells.shape[dim], axis=dim)
        cells = jnp.concatenate(
            [
                lax.ppermute(tail, axis, [(i, (i + 1) % count) for i in range(ends)]),
                cells,
                lax.ppermute(head, axis, [((i + 1) % count, i) for i in range(ends)]),
            ],
            axis=dim,
        )
    return cells


def basis_table(mode_total, length):
    mode_index = jnp.arange(mode_total, dtype=jnp.float32)[:, None]
    cell_index = jnp.arange(length, dtype=jnp.float32)[None, :]
    phase_angle = math.pi / (2.0 * length) * mode_index * (2.0 * cell_index + 1.0)
    amplitude = jnp.where(mode_index == 0.0, math.sqrt(1.0 / length), math.sqrt(2.0 / length))
    return (amplitude * jnp.cos(phase_angle)).astype(jnp.bfloat16)


def pencil_work(pencil, spec_weight, kept_modes, adjoint):
    basis = basis_table(spec_weight.shape[0], pencil.shape[0])
    coefficients = jnp.einsum(
        "kx,xycz->kycz", basis, pencil, preferred_element_type=jnp.float32
    ).astype(jnp.bfloat16)
    if adjoint:
        masked = coefficients * kept_modes[:, None, :, None].astype(jnp.bfloat16)
        mixed_modes = jnp.einsum(
            "koc,kyoz->kycz", spec_weight, masked, preferred_element_type=jnp.float32
        ).astype(jnp.bfloat16)
    else:
        mixed_modes = jnp.einsum(
            "koc,kycz->kyoz", spec_weight, coefficients, preferred_element_type=jnp.float32
        )
        mixed_modes = (mixed_modes * kept_modes[:, None, :, None]).astype(jnp.bfloat16)
    return jnp.einsum(
        "kx,kyoz->xyoz", basis, mixed_modes, preferred_element_type=jnp.float32
    ).astype(jnp.bfloat16)


def spectral(slab, spec_weight, kept_modes, adjoint):
    result = pencil_work(
        lax.all_to_all(slab, "gx", split_axis=1, concat_axis=0, tiled=True),
        spec_weight,
        kept_modes,
        adjoint,
    )
    return lax.all_to_all(result, "gx", split_axis=0, concat_axis=1, tiled=True)


def laplace_ext(extended):
    padded = jnp.pad(extended, ((0, 0), (1, 1), (0, 0), (1, 1))).astype(jnp.float32)
    centre_cells = padded[1:-1, 1:-1, :, 1:-1]
    neighbours = padded[2:, 1:-1, :, 1:-1] + padded[:-2, 1:-1, :, 1:-1]
    neighbours = neighbours + padded[1:-1, 2:, :, 1:-1] + padded[1:-1, :-2, :, 1:-1]
    neighbours = neighbours + padded[1:-1, 1:-1, :, 2:] + padded[1:-1, 1:-1, :, :-2]
    return (neighbours - 6.0 * centre_cells).astype(jnp.bfloat16)


def pad_sides(extended):
    return jnp.pad(extended, ((0, 0), (RAD, RAD), (0, 0), (RAD, RAD)))


def window_of(padded, offset, direction, slab_shape):
    starts = (
        1 + direction * offset[0],
        RAD + direction * offset[1],
        0,
        RAD + direction * offset[2],
    )
    return lax.dynamic_slice(padded, starts, slab_shape)


def gelu_slope(preact, upstream):
    _, pullback = jax.vjp(partial(jax.nn.gelu, approximate=True), preact)
    return pullback(upstream)[0]


def sum_over_gx(terms):
    count = lax.axis_size("gx")
    if terms.size % count:
        return lax.psum(terms, "gx")
    pieces = lax.all_to_all(terms.reshape(count, -1), "gx", split_axis=0, concat_axis=0, tiled=True)
    mine = jnp.sum(pieces, axis=0)
    copies = jnp.broadcast_to(mine[None, :], pieces.shape)
    gathered = lax.all_to_all(copies, "gx", split_axis=0, concat_axis=0, tiled=True)
    return gathered.reshape(terms.shape)


def per_device(
    features,
    cotangent,
    wall_flags,
    mode_counts,
    offsets,
    point_weight,
    kernel_weight,
    lap_weight,
    spec_weight,
    bias,
):
    mode_total = spec_weight.shape[0]
    tile_total = kernel_weight.shape[0]
    kept_modes = (jnp.arange(mode_total, dtype=jnp.int32)[:, None] < mode_counts[None, :]).astype(
        jnp.float32
    )
    fluid_mask = (1 - wall_flags).astype(jnp.float32)[:, :, None, :]
    extended = with_halo(features, (("gx", 0),), 1)
    padded_field = pad_sides(extended)
    local_part = jnp.einsum(
        "oc,xycz->xyoz", point_weight, features, preferred_element_type=jnp.float32
    )
    local_part = local_part + jnp.einsum(
        "oc,xycz->xyoz", lap_weight, laplace_ext(extended), preferred_element_type=jnp.float32
    )
    for tile in range(tile_total):
        moved = window_of(padded_field, offsets[tile], 1, features.shape)
        local_part = local_part + jnp.einsum(
            "oc,xycz->xyoz", kernel_weight[tile], moved, preferred_element_type=jnp.float32
        )
    local_part = local_part + bias[:, None]
    spectral_part = spectral(features, spec_weight, kept_modes, False)
    preact = local_part + spectral_part.astype(jnp.float32)
    weighted = (gelu_slope(preact, cotangent.astype(jnp.float32)) * fluid_mask).astype(jnp.bfloat16)
    spec_grad = spectral(weighted, spec_weight, kept_modes, True)
    ext_grad = with_halo(weighted, (("gx", 0),), 1)
    padded_grad = pad_sides(ext_grad)
    input_grad = jnp.einsum(
        "oc,xyoz->xycz", point_weight, weighted, preferred_element_type=jnp.float32
    )
    input_grad = input_grad + jnp.einsum(
        "oc,xyoz->xycz", lap_weight, laplace_ext(ext_grad), preferred_element_type=jnp.float32
    )
    input_grad = input_grad + spec_grad.astype(jnp.float32)
    tile_grads = []
    for tile in range(tile_total):
        back_moved = window_of(padded_grad, offsets[tile], -1, weighted.shape)
        input_grad = input_grad + jnp.einsum(
            "oc,xyoz->xycz", kernel_weight[tile], back_moved, preferred_element_type=jnp.float32
        )
        tile_grads.append(
            jnp.einsum("xyoz,xycz->oc", back_moved, features, preferred_element_type=jnp.float32)
        )
    local_grad = jnp.stack(tile_grads, axis=0)
    scaling = float(
        lax.axis_size("gx") * features.shape[0] * features.shape[1] * features.shape[3]
    ) ** (-0.5)
    summed = sum_over_gx(local_grad)
    return (input_grad.astype(jnp.bfloat16), summed * scaling)


def fused_kernel(
    count,
    feat,
    cot,
    wall,
    offs,
    basis,
    wf,
    wb,
    wm,
    wmt,
    bias,
    out,
    kout,
    zs,
    cat,
    local,
    acc,
    vh,
    pen1,
    pen2,
    stage1,
    stage2,
    spec1,
    spec2,
    wgt,
    halo1,
    halo2,
    kacc,
    kpart,
    ksum,
    kall,
    shift,
    send,
    recv,
    hsend,
    hrecv,
):
    me = lax.axis_index("gx")
    grp = lax.axis_index("groups")
    xl, ny, ch, nz = feat.shape
    modes = wm.shape[0]
    tiles = offs.shape[0]
    f32, bf16 = jnp.float32, jnp.bfloat16

    def remote(src, dst, phase, d, peer):
        return pltpu.make_async_remote_copy(
            src_ref=src,
            dst_ref=dst,
            send_sem=send.at[phase, d],
            recv_sem=recv.at[phase, d],
            device_id=(grp, peer),
            device_id_type=MESH,
        )

    def ahead(d):
        return lax.rem(me + d, count)

    def behind(d):
        return lax.rem(me + count - d, count)

    def halo_copy(src, dst, slot, peer):
        return pltpu.make_async_remote_copy(
            src_ref=src,
            dst_ref=dst,
            send_sem=hsend.at[slot],
            recv_sem=hrecv.at[slot],
            device_id=(grp, peer),
            device_id_type=MESH,
        )

    def each(low, high, body):
        def step(i, carry):
            body(i)
            return carry

        lax.fori_loop(low, high, step, 0)

    from_z = lax.broadcasted_iota(jnp.int32, (nz, nz), 0)
    to_z = lax.broadcasted_iota(jnp.int32, (nz, nz), 1)
    for m, dz in enumerate([dz for dz in range(-RAD, RAD + 1) if dz]):
        shift[:, m * nz : (m + 1) * nz] = jnp.where(from_z == to_z + dz, 1.0, 0.0).astype(bf16)

    barrier = pltpu.get_barrier_semaphore()
    each(
        1,
        count,
        lambda d: pl.semaphore_signal(
            barrier, inc=1, device_id=(grp, ahead(d)), device_id_type=MESH
        ),
    )
    pl.semaphore_wait(barrier, count - 1)

    def halo_start(low_plane, high_plane, halo, base):
        @pl.when(me > 0)
        def _():
            halo_copy(low_plane, halo.at[1], base, me - 1).start()

        @pl.when(me < count - 1)
        def _():
            halo_copy(high_plane, halo.at[0], base + 1, me + 1).start()

        @pl.when(me == 0)
        def _():
            halo[0] = jnp.zeros(halo.shape[1:], bf16)

        @pl.when(me == count - 1)
        def _():
            halo[1] = jnp.zeros(halo.shape[1:], bf16)

    def halo_wait(low_plane, high_plane, halo, base):
        @pl.when(me > 0)
        def _():
            halo_copy(low_plane, halo.at[1], base, me - 1).wait_send()
            halo_copy(high_plane, halo.at[0], base + 1, me - 1).wait_recv()

        @pl.when(me < count - 1)
        def _():
            halo_copy(high_plane, halo.at[0], base + 1, me + 1).wait_send()
            halo_copy(low_plane, halo.at[1], base, me + 1).wait_recv()

    moves = [dz for dz in range(-RAD, RAD + 1) if dz]
    group = math.gcd(ny, 8)

    def spread(load, place):
        def body(i):
            y = i * group
            v = load(pl.ds(y, group))
            zs[RAD, place, pl.ds(y + RAD, group)] = v
            flat = v.reshape(group * ch, nz)
            moved = jnp.dot(flat, shift[...], preferred_element_type=f32).astype(bf16)
            for m, dz in enumerate(moves):
                piece = moved[:, m * nz : (m + 1) * nz].reshape(group, ch, nz)
                zs[RAD + dz, place, pl.ds(y + RAD, group)] = piece

        each(0, ny // group, body)

    def gather_rows(direction):
        def body(y):
            for x in range(xl):
                lanes = slice(x * nz, (x + 1) * nz)
                centre = zs[RAD, x + 1, y + RAD]
                cat[y, 0:ch, lanes] = centre
                total = zs[RAD, x + 2, y + RAD].astype(f32) + zs[RAD, x, y + RAD].astype(f32)
                total = total + zs[RAD, x + 1, y + RAD + 1].astype(f32)
                total = total + zs[RAD, x + 1, y + RAD - 1].astype(f32)
                total = total + zs[RAD + 1, x + 1, y + RAD].astype(f32)
                total = total + zs[RAD - 1, x + 1, y + RAD].astype(f32)
                cat[y, ch : 2 * ch, lanes] = (total - 6.0 * centre.astype(f32)).astype(bf16)
                for t in range(tiles):
                    moved = zs[
                        RAD + direction * offs[t, 2],
                        x + 1 + direction * offs[t, 0],
                        y + RAD + direction * offs[t, 1],
                    ]
                    cat[y, (2 + t) * ch : (3 + t) * ch, lanes] = moved

        each(0, ny, body)

    unroll = math.gcd(ny, 4)

    def each_row(body):
        def rows_at(i):
            for r in range(unroll):
                body(i * unroll + r)

        each(0, ny // unroll, rows_at)

    def mix(weights):
        def body(y):
            local[y] = jnp.dot(weights[...], cat[y], preferred_element_type=f32)

        each_row(body)

    def gain(planes, src):
        wide = [p.astype(f32) for p in planes]
        for k in range(modes):
            total = acc[k]
            for j in range(xl):
                total = total + basis[k, src * xl + j] * wide[j]
            acc[k] = total

    def channel_mix(weights):
        for k in range(modes):
            u = acc[k].astype(bf16)
            v = jnp.dot(weights[k], u, preferred_element_type=f32)
            vh[k] = v.astype(bf16).astype(f32)

    def expand(stage, peer):
        for j in range(xl):
            total = basis[0, peer * xl + j] * vh[0]
            for k in range(1, modes):
                total = total + basis[k, peer * xl + j] * vh[k]
            stage[peer, j] = total.astype(bf16)

    def each_peer(body):
        half = count // 2
        each(1, count, lambda i: body(half + (i // 2) * (1 - 2 * lax.rem(i, 2))))

    each_peer(lambda d: remote(feat.at[:, ahead(d)], pen1.at[me], 0, d, ahead(d)).start())
    low1, high1 = feat.at[0], feat.at[xl - 1]
    halo_start(low1, high1, halo1, 0)

    for edge in (0, RAD + ny):
        for dz in range(2 * RAD + 1):
            for x in range(xl + 2):
                zs[dz, x, edge : edge + RAD] = jnp.zeros((RAD, ch, nz), bf16)
    for x in range(xl):
        spread(lambda y: feat[x, y], x + 1)
    acc[...] = jnp.zeros(acc.shape, f32)
    gain([feat[j, me] for j in range(xl)], me)

    def take1(d):
        src = behind(d)
        remote(feat.at[:, src], pen1.at[src], 0, d, src).wait_recv()
        gain([pen1[src, j] for j in range(xl)], src)

    each_peer(take1)
    channel_mix(wm)

    def give1(d):
        peer = ahead(d)
        expand(stage1, peer)
        remote(stage1.at[peer], spec1.at[me], 1, d, peer).start()

    each_peer(give1)
    expand(stage1, me)
    halo_wait(low1, high1, halo1, 0)
    spread(lambda y: halo1[0, y], 0)
    spread(lambda y: halo1[1, y], xl + 1)
    gather_rows(1)
    mix(wf)
    root = math.sqrt(2.0 / math.pi)

    def slope(y, planes):
        for x in range(xl):
            v = local[y, :, x * nz : (x + 1) * nz] + planes[x].astype(f32) + bias[...]
            square = v * v
            t = jnp.tanh(root * (v + 0.044715 * (square * v)))
            g = 0.5 * (1.0 + t)
            g = g + (0.5 * v) * ((1.0 - t * t) * (root * (1.0 + (3.0 * 0.044715) * square)))
            fluid = (1 - wall[x, pl.ds(y, 1), :]).astype(f32)
            wgt[y, x] = ((cot[x, y].astype(f32) * g) * fluid).astype(bf16)

    slope(me, [stage1[me, j] for j in range(xl)])

    def turn(d):
        src = behind(d)
        remote(stage1.at[src], spec1.at[src], 1, d, src).wait_recv()
        slope(src, [spec1[src, j] for j in range(xl)])

    each_peer(turn)

    low2, high2 = wgt.at[:, 0], wgt.at[:, xl - 1]
    halo_start(low2, high2, halo2, 2)
    each_peer(lambda d: remote(wgt.at[ahead(d)], pen2.at[me], 2, d, ahead(d)).start())
    for x in range(xl):
        spread(lambda y: wgt[y, x], x + 1)
    acc[...] = jnp.zeros(acc.shape, f32)
    gain([wgt[me, j] for j in range(xl)], me)
    halo_wait(low2, high2, halo2, 2)
    spread(lambda y: halo2[0, y], 0)
    spread(lambda y: halo2[1, y], xl + 1)
    gather_rows(-1)

    kacc[...] = jnp.zeros(kacc.shape, f32)

    def tile_grad(y):
        field = jnp.concatenate([feat[x, y] for x in range(xl)], axis=1)
        kacc[...] += lax.dot_general(
            cat[y, 2 * ch :, :], field, (((1,), (1,)), ((), ())), preferred_element_type=f32
        )

    each_row(tile_grad)
    rows = kpart.shape[1]
    for p in range(count):
        kpart[p] = kacc[p * rows : (p + 1) * rows]
    each_peer(lambda d: remote(kpart.at[ahead(d)], ksum.at[me], 4, d, ahead(d)).start())

    def take2(d):
        src = behind(d)
        remote(wgt.at[src], pen2.at[src], 2, d, src).wait_recv()
        gain([pen2[src, j] for j in range(xl)], src)

    each_peer(take2)
    ksum[me] = kpart[me]
    each_peer(lambda d: remote(kpart.at[0], ksum.at[behind(d)], 4, d, behind(d)).wait_recv())
    total = ksum[0]
    for p in range(1, count):
        total = total + ksum[p]
    kall[me] = total * (float(count * xl * ny * nz) ** -0.5)
    each_peer(lambda d: remote(kall.at[me], kall.at[me], 5, d, ahead(d)).start())
    channel_mix(wmt)

    def give2(d):
        peer = ahead(d)
        expand(stage2, peer)
        remote(stage2.at[peer], spec2.at[me], 3, d, peer).start()

    each_peer(give2)
    expand(stage2, me)

    mix(wb)

    def finish(y, planes):
        for x in range(xl):
            total = local[y, :, x * nz : (x + 1) * nz] + planes[x].astype(f32)
            out[x, y] = total.astype(bf16)

    finish(me, [stage2[me, j] for j in range(xl)])

    def last(d):
        src = behind(d)
        remote(stage2.at[src], spec2.at[src], 3, d, src).wait_recv()
        finish(src, [spec2[src, j] for j in range(xl)])

    each_peer(last)
    each_peer(lambda d: remote(kall.at[me], kall.at[behind(d)], 5, d, behind(d)).wait_recv())
    kout[...] = kall[...]

    def drain(d):
        peer = ahead(d)
        remote(feat.at[:, peer], pen1.at[me], 0, d, peer).wait_send()
        remote(stage1.at[peer], spec1.at[me], 1, d, peer).wait_send()
        remote(wgt.at[peer], pen2.at[me], 2, d, peer).wait_send()
        remote(stage2.at[peer], spec2.at[me], 3, d, peer).wait_send()
        remote(kpart.at[peer], ksum.at[me], 4, d, peer).wait_send()
        remote(kall.at[me], kall.at[me], 5, d, peer).wait_send()

    each_peer(drain)


def fits_kernel(count, features, kernel_weight):
    xl, ny, ch, nz = features.shape
    cells = xl * ny * ch * nz
    tile_rows = kernel_weight.shape[0] * ch
    if ny != count or nz % 128 or ch % 16 or tile_rows % (8 * count):
        return False
    return 80 * cells < 24 * 2**20


def fused_device(
    features,
    cotangent,
    wall_flags,
    mode_counts,
    offsets,
    point_weight,
    kernel_weight,
    lap_weight,
    spec_weight,
    bias,
):
    count = lax.axis_size("gx")
    if not fits_kernel(count, features, kernel_weight):
        return per_device(
            features,
            cotangent,
            wall_flags,
            mode_counts,
            offsets,
            point_weight,
            kernel_weight,
            lap_weight,
            spec_weight,
            bias,
        )
    xl, ny, ch, nz = features.shape
    modes, tiles = spec_weight.shape[0], kernel_weight.shape[0]
    kept = jnp.arange(modes, dtype=jnp.int32)[:, None] < mode_counts[None, :]
    masked = jnp.where(kept[:, :, None], spec_weight, jnp.zeros_like(spec_weight))
    stacked = jnp.concatenate([point_weight[None], lap_weight[None], kernel_weight], axis=0)
    forward = jnp.transpose(stacked, (1, 0, 2)).reshape(ch, (2 + tiles) * ch)
    backward = jnp.transpose(stacked, (2, 0, 1)).reshape(ch, (2 + tiles) * ch)
    rows = tiles * ch // count
    f32, bf16 = jnp.float32, jnp.bfloat16
    vmem = pl.BlockSpec(memory_space=pltpu.VMEM)
    smem = pl.BlockSpec(memory_space=pltpu.SMEM)
    field_grad, tile_grad = pl.pallas_call(
        functools.partial(fused_kernel, count),
        out_shape=(
            jax.ShapeDtypeStruct(features.shape, bf16),
            jax.ShapeDtypeStruct((count, rows, ch), f32),
        ),
        in_specs=[vmem, vmem, vmem, smem, smem, vmem, vmem, vmem, vmem, vmem],
        out_specs=(vmem, vmem),
        scratch_shapes=[
            pltpu.VMEM((2 * RAD + 1, xl + 2, ny + 2 * RAD, ch, nz), bf16),
            pltpu.VMEM((ny, (2 + tiles) * ch, xl * nz), bf16),
            pltpu.VMEM((ny, ch, xl * nz), f32),
            pltpu.VMEM((modes, ch, nz), f32),
            pltpu.VMEM((modes, ch, nz), f32),
            pltpu.VMEM((count, xl, ch, nz), bf16),
            pltpu.VMEM((count, xl, ch, nz), bf16),
            pltpu.VMEM((count, xl, ch, nz), bf16),
            pltpu.VMEM((count, xl, ch, nz), bf16),
            pltpu.VMEM((count, xl, ch, nz), bf16),
            pltpu.VMEM((count, xl, ch, nz), bf16),
            pltpu.VMEM((ny, xl, ch, nz), bf16),
            pltpu.VMEM((2, ny, ch, nz), bf16),
            pltpu.VMEM((2, ny, ch, nz), bf16),
            pltpu.VMEM((tiles * ch, ch), f32),
            pltpu.VMEM((count, rows, ch), f32),
            pltpu.VMEM((count, rows, ch), f32),
            pltpu.VMEM((count, rows, ch), f32),
            pltpu.VMEM((nz, 2 * RAD * nz), bf16),
            pltpu.SemaphoreType.DMA((6, count)),
            pltpu.SemaphoreType.DMA((6, count)),
            pltpu.SemaphoreType.DMA((4,)),
            pltpu.SemaphoreType.DMA((4,)),
        ],
        compiler_params=pltpu.CompilerParams(
            collective_id=0, has_side_effects=True, vmem_limit_bytes=48 * 2**20
        ),
    )(
        features,
        cotangent,
        wall_flags,
        offsets,
        basis_table(modes, count * xl).astype(f32),
        forward,
        backward,
        masked,
        jnp.swapaxes(masked, 1, 2),
        jnp.broadcast_to(bias[:, None], (ch, nz)),
    )
    return field_grad, tile_grad.reshape(kernel_weight.shape)


def solution(mesh):
    return jax.shard_map(
        fused_device,
        mesh=mesh,
        in_specs=(
            P(("groups", "gx"), None, None, None),
            P(("groups", "gx"), None, None, None),
            P(("groups", "gx"), None, None),
            P(),
            P(),
            P(),
            P(),
            P(),
            P(),
            P(),
        ),
        out_specs=(P(("groups", "gx"), None, None, None), P("groups", None, None)),
        check_vma=False,
    )
```

```python
import functools
from functools import partial
import math

import jax
import jax.numpy as jnp
from jax import lax
from jax.experimental import pallas as pl
from jax.experimental.pallas import tpu as pltpu
from jax.sharding import PartitionSpec as P

RAD = 2
MESH = pl.DeviceIdType.MESH


def with_halo(cells, sides, width):
    for axis, dim in sides:
        count = lax.axis_size(axis)
        ends = count - 1
        head = lax.slice_in_dim(cells, 0, width, axis=dim)
        tail = lax.slice_in_dim(cells, cells.shape[dim] - width, cells.shape[dim], axis=dim)
        cells = jnp.concatenate(
            [
                lax.ppermute(tail, axis, [(i, (i + 1) % count) for i in range(ends)]),
                cells,
                lax.ppermute(head, axis, [((i + 1) % count, i) for i in range(ends)]),
            ],
            axis=dim,
        )
    return cells


def basis_table(mode_total, length):
    mode_index = jnp.arange(mode_total, dtype=jnp.float32)[:, None]
    cell_index = jnp.arange(length, dtype=jnp.float32)[None, :]
    phase_angle = math.pi / (2.0 * length) * mode_index * (2.0 * cell_index + 1.0)
    amplitude = jnp.where(mode_index == 0.0, math.sqrt(1.0 / length), math.sqrt(2.0 / length))
    return (amplitude * jnp.cos(phase_angle)).astype(jnp.bfloat16)


def pencil_work(pencil, spec_weight, kept_modes, adjoint):
    basis = basis_table(spec_weight.shape[0], pencil.shape[0])
    coefficients = jnp.einsum(
        "kx,xycz->kycz", basis, pencil, preferred_element_type=jnp.float32
    ).astype(jnp.bfloat16)
    if adjoint:
        masked = coefficients * kept_modes[:, None, :, None].astype(jnp.bfloat16)
        mixed_modes = jnp.einsum(
            "koc,kyoz->kycz", spec_weight, masked, preferred_element_type=jnp.float32
        ).astype(jnp.bfloat16)
    else:
        mixed_modes = jnp.einsum(
            "koc,kycz->kyoz", spec_weight, coefficients, preferred_element_type=jnp.float32
        )
        mixed_modes = (mixed_modes * kept_modes[:, None, :, None]).astype(jnp.bfloat16)
    return jnp.einsum(
        "kx,kyoz->xyoz", basis, mixed_modes, preferred_element_type=jnp.float32
    ).astype(jnp.bfloat16)


def spectral(slab, spec_weight, kept_modes, adjoint):
    result = pencil_work(
        lax.all_to_all(slab, "gx", split_axis=1, concat_axis=0, tiled=True),
        spec_weight,
        kept_modes,
        adjoint,
    )
    return lax.all_to_all(result, "gx", split_axis=0, concat_axis=1, tiled=True)


def laplace_ext(extended):
    padded = jnp.pad(extended, ((0, 0), (1, 1), (0, 0), (1, 1))).astype(jnp.float32)
    centre_cells = padded[1:-1, 1:-1, :, 1:-1]
    neighbours = padded[2:, 1:-1, :, 1:-1] + padded[:-2, 1:-1, :, 1:-1]
    neighbours = neighbours + padded[1:-1, 2:, :, 1:-1] + padded[1:-1, :-2, :, 1:-1]
    neighbours = neighbours + padded[1:-1, 1:-1, :, 2:] + padded[1:-1, 1:-1, :, :-2]
    return (neighbours - 6.0 * centre_cells).astype(jnp.bfloat16)


def pad_sides(extended):
    return jnp.pad(extended, ((0, 0), (RAD, RAD), (0, 0), (RAD, RAD)))


def window_of(padded, offset, direction, slab_shape):
    starts = (
        1 + direction * offset[0],
        RAD + direction * offset[1],
        0,
        RAD + direction * offset[2],
    )
    return lax.dynamic_slice(padded, starts, slab_shape)


def gelu_slope(preact, upstream):
    _, pullback = jax.vjp(partial(jax.nn.gelu, approximate=True), preact)
    return pullback(upstream)[0]


def sum_over_gx(terms):
    count = lax.axis_size("gx")
    if terms.size % count:
        return lax.psum(terms, "gx")
    pieces = lax.all_to_all(terms.reshape(count, -1), "gx", split_axis=0, concat_axis=0, tiled=True)
    mine = jnp.sum(pieces, axis=0)
    copies = jnp.broadcast_to(mine[None, :], pieces.shape)
    gathered = lax.all_to_all(copies, "gx", split_axis=0, concat_axis=0, tiled=True)
    return gathered.reshape(terms.shape)


def per_device(
    features,
    cotangent,
    wall_flags,
    mode_counts,
    offsets,
    point_weight,
    kernel_weight,
    lap_weight,
    spec_weight,
    bias,
):
    mode_total = spec_weight.shape[0]
    tile_total = kernel_weight.shape[0]
    kept_modes = (jnp.arange(mode_total, dtype=jnp.int32)[:, None] < mode_counts[None, :]).astype(
        jnp.float32
    )
    fluid_mask = (1 - wall_flags).astype(jnp.float32)[:, :, None, :]
    extended = with_halo(features, (("gx", 0),), 1)
    padded_field = pad_sides(extended)
    local_part = jnp.einsum(
        "oc,xycz->xyoz", point_weight, features, preferred_element_type=jnp.float32
    )
    local_part = local_part + jnp.einsum(
        "oc,xycz->xyoz", lap_weight, laplace_ext(extended), preferred_element_type=jnp.float32
    )
    for tile in range(tile_total):
        moved = window_of(padded_field, offsets[tile], 1, features.shape)
        local_part = local_part + jnp.einsum(
            "oc,xycz->xyoz", kernel_weight[tile], moved, preferred_element_type=jnp.float32
        )
    local_part = local_part + bias[:, None]
    spectral_part = spectral(features, spec_weight, kept_modes, False)
    preact = local_part + spectral_part.astype(jnp.float32)
    weighted = (gelu_slope(preact, cotangent.astype(jnp.float32)) * fluid_mask).astype(jnp.bfloat16)
    spec_grad = spectral(weighted, spec_weight, kept_modes, True)
    ext_grad = with_halo(weighted, (("gx", 0),), 1)
    padded_grad = pad_sides(ext_grad)
    input_grad = jnp.einsum(
        "oc,xyoz->xycz", point_weight, weighted, preferred_element_type=jnp.float32
    )
    input_grad = input_grad + jnp.einsum(
        "oc,xyoz->xycz", lap_weight, laplace_ext(ext_grad), preferred_element_type=jnp.float32
    )
    input_grad = input_grad + spec_grad.astype(jnp.float32)
    tile_grads = []
    for tile in range(tile_total):
        back_moved = window_of(padded_grad, offsets[tile], -1, weighted.shape)
        input_grad = input_grad + jnp.einsum(
            "oc,xyoz->xycz", kernel_weight[tile], back_moved, preferred_element_type=jnp.float32
        )
        tile_grads.append(
            jnp.einsum("xyoz,xycz->oc", back_moved, features, preferred_element_type=jnp.float32)
        )
    local_grad = jnp.stack(tile_grads, axis=0)
    scaling = float(
        lax.axis_size("gx") * features.shape[0] * features.shape[1] * features.shape[3]
    ) ** (-0.5)
    summed = sum_over_gx(local_grad)
    return (input_grad.astype(jnp.bfloat16), summed * scaling)


def fused_kernel(
    count,
    feat,
    cot,
    wall,
    offs,
    basis,
    wf,
    wb,
    wm,
    wmt,
    bias,
    out,
    kout,
    zs,
    cat,
    local,
    acc,
    vh,
    pen1,
    pen2,
    stage1,
    stage2,
    spec1,
    spec2,
    wgt,
    halo1,
    halo2,
    kacc,
    kpart,
    ksum,
    kall,
    shift,
    send,
    recv,
    hsend,
    hrecv,
):
    me = lax.axis_index("gx")
    grp = lax.axis_index("groups")
    xl, ny, ch, nz = feat.shape
    modes = wm.shape[0]
    tiles = offs.shape[0]
    f32, bf16 = jnp.float32, jnp.bfloat16

    def remote(src, dst, phase, d, peer):
        return pltpu.make_async_remote_copy(
            src_ref=src,
            dst_ref=dst,
            send_sem=send.at[phase, d],
            recv_sem=recv.at[phase, d],
            device_id=(grp, peer),
            device_id_type=MESH,
        )

    def ahead(d):
        return lax.rem(me + d, count)

    def behind(d):
        return lax.rem(me + count - d, count)

    def halo_copy(src, dst, slot, peer):
        return pltpu.make_async_remote_copy(
            src_ref=src,
            dst_ref=dst,
            send_sem=hsend.at[slot],
            recv_sem=hrecv.at[slot],
            device_id=(grp, peer),
            device_id_type=MESH,
        )

    def each(low, high, body):
        def step(i, carry):
            body(i)
            return carry

        lax.fori_loop(low, high, step, 0)

    from_z = lax.broadcasted_iota(jnp.int32, (nz, nz), 0)
    to_z = lax.broadcasted_iota(jnp.int32, (nz, nz), 1)
    for m, dz in enumerate([dz for dz in range(-RAD, RAD + 1) if dz]):
        shift[:, m * nz : (m + 1) * nz] = jnp.where(from_z == to_z + dz, 1.0, 0.0).astype(bf16)

    barrier = pltpu.get_barrier_semaphore()
    each(
        1,
        count,
        lambda d: pl.semaphore_signal(
            barrier, inc=1, device_id=(grp, ahead(d)), device_id_type=MESH
        ),
    )
    pl.semaphore_wait(barrier, count - 1)

    def halo_start(low_plane, high_plane, halo, base):
        @pl.when(me > 0)
        def _():
            halo_copy(low_plane, halo.at[1], base, me - 1).start()

        @pl.when(me < count - 1)
        def _():
            halo_copy(high_plane, halo.at[0], base + 1, me + 1).start()

        @pl.when(me == 0)
        def _():
            halo[0] = jnp.zeros(halo.shape[1:], bf16)

        @pl.when(me == count - 1)
        def _():
            halo[1] = jnp.zeros(halo.shape[1:], bf16)

    def halo_wait(low_plane, high_plane, halo, base):
        @pl.when(me > 0)
        def _():
            halo_copy(low_plane, halo.at[1], base, me - 1).wait_send()
            halo_copy(high_plane, halo.at[0], base + 1, me - 1).wait_recv()

        @pl.when(me < count - 1)
        def _():
            halo_copy(high_plane, halo.at[0], base + 1, me + 1).wait_send()
            halo_copy(low_plane, halo.at[1], base, me + 1).wait_recv()

    moves = [dz for dz in range(-RAD, RAD + 1) if dz]
    group = math.gcd(ny, 8)

    def spread(load, place):
        def body(i):
            y = i * group
            v = load(pl.ds(y, group))
            zs[RAD, place, pl.ds(y + RAD, group)] = v
            flat = v.reshape(group * ch, nz)
            moved = jnp.dot(flat, shift[...], preferred_element_type=f32).astype(bf16)
            for m, dz in enumerate(moves):
                piece = moved[:, m * nz : (m + 1) * nz].reshape(group, ch, nz)
                zs[RAD + dz, place, pl.ds(y + RAD, group)] = piece

        each(0, ny // group, body)

    def gather_rows(direction):
        def body(y):
            for x in range(xl):
                lanes = slice(x * nz, (x + 1) * nz)
                centre = zs[RAD, x + 1, y + RAD]
                cat[y, 0:ch, lanes] = centre
                total = zs[RAD, x + 2, y + RAD].astype(f32) + zs[RAD, x, y + RAD].astype(f32)
                total = total + zs[RAD, x + 1, y + RAD + 1].astype(f32)
                total = total + zs[RAD, x + 1, y + RAD - 1].astype(f32)
                total = total + zs[RAD + 1, x + 1, y + RAD].astype(f32)
                total = total + zs[RAD - 1, x + 1, y + RAD].astype(f32)
                cat[y, ch : 2 * ch, lanes] = (total - 6.0 * centre.astype(f32)).astype(bf16)
                for t in range(tiles):
                    moved = zs[
                        RAD + direction * offs[t, 2],
                        x + 1 + direction * offs[t, 0],
                        y + RAD + direction * offs[t, 1],
                    ]
                    cat[y, (2 + t) * ch : (3 + t) * ch, lanes] = moved

        each(0, ny, body)

    unroll = math.gcd(ny, 4)

    def each_row(body):
        def rows_at(i):
            for r in range(unroll):
                body(i * unroll + r)

        each(0, ny // unroll, rows_at)

    def mix(weights):
        def body(y):
            local[y] = jnp.dot(weights[...], cat[y], preferred_element_type=f32)

        each_row(body)

    def gain(planes, src):
        wide = [p.astype(f32) for p in planes]
        for k in range(modes):
            total = acc[k]
            for j in range(xl):
                total = total + basis[k, src * xl + j] * wide[j]
            acc[k] = total

    def channel_mix(weights):
        for k in range(modes):
            u = acc[k].astype(bf16)
            v = jnp.dot(weights[k], u, preferred_element_type=f32)
            vh[k] = v.astype(bf16).astype(f32)

    def expand(stage, peer):
        for j in range(xl):
            total = basis[0, peer * xl + j] * vh[0]
            for k in range(1, modes):
                total = total + basis[k, peer * xl + j] * vh[k]
            stage[peer, j] = total.astype(bf16)

    def each_peer(body):
        half = count // 2
        each(1, count, lambda i: body(half + (i // 2) * (1 - 2 * lax.rem(i, 2))))

    each_peer(lambda d: remote(feat.at[:, ahead(d)], pen1.at[me], 0, d, ahead(d)).start())
    low1, high1 = feat.at[0], feat.at[xl - 1]
    halo_start(low1, high1, halo1, 0)

    for edge in (0, RAD + ny):
        for dz in range(2 * RAD + 1):
            for x in range(xl + 2):
                zs[dz, x, edge : edge + RAD] = jnp.zeros((RAD, ch, nz), bf16)
    for x in range(xl):
        spread(lambda y: feat[x, y], x + 1)
    acc[...] = jnp.zeros(acc.shape, f32)
    gain([feat[j, me] for j in range(xl)], me)

    def take1(d):
        src = behind(d)
        remote(feat.at[:, src], pen1.at[src], 0, d, src).wait_recv()
        gain([pen1[src, j] for j in range(xl)], src)

    each_peer(take1)
    channel_mix(wm)

    def give1(d):
        peer = ahead(d)
        expand(stage1, peer)
        remote(stage1.at[peer], spec1.at[me], 1, d, peer).start()

    each_peer(give1)
    expand(stage1, me)
    halo_wait(low1, high1, halo1, 0)
    spread(lambda y: halo1[0, y], 0)
    spread(lambda y: halo1[1, y], xl + 1)
    gather_rows(1)
    mix(wf)
    root = math.sqrt(2.0 / math.pi)

    def slope(y, planes):
        for x in range(xl):
            v = local[y, :, x * nz : (x + 1) * nz] + planes[x].astype(f32) + bias[...]
            square = v * v
            t = jnp.tanh(root * (v + 0.044715 * (square * v)))
            g = 0.5 * (1.0 + t)
            g = g + (0.5 * v) * ((1.0 - t * t) * (root * (1.0 + (3.0 * 0.044715) * square)))
            fluid = (1 - wall[x, pl.ds(y, 1), :]).astype(f32)
            wgt[y, x] = ((cot[x, y].astype(f32) * g) * fluid).astype(bf16)

    slope(me, [stage1[me, j] for j in range(xl)])

    def turn(d):
        src = behind(d)
        remote(stage1.at[src], spec1.at[src], 1, d, src).wait_recv()
        slope(src, [spec1[src, j] for j in range(xl)])

    each_peer(turn)

    low2, high2 = wgt.at[:, 0], wgt.at[:, xl - 1]
    halo_start(low2, high2, halo2, 2)
    each_peer(lambda d: remote(wgt.at[ahead(d)], pen2.at[me], 2, d, ahead(d)).start())
    for x in range(xl):
        spread(lambda y: wgt[y, x], x + 1)
    acc[...] = jnp.zeros(acc.shape, f32)
    gain([wgt[me, j] for j in range(xl)], me)
    halo_wait(low2, high2, halo2, 2)
    spread(lambda y: halo2[0, y], 0)
    spread(lambda y: halo2[1, y], xl + 1)
    gather_rows(-1)

    kacc[...] = jnp.zeros(kacc.shape, f32)

    def tile_grad(y):
        field = jnp.concatenate([feat[x, y] for x in range(xl)], axis=1)
        kacc[...] += lax.dot_general(
            cat[y, 2 * ch :, :], field, (((1,), (1,)), ((), ())), preferred_element_type=f32
        )

    each_row(tile_grad)
    rows = kpart.shape[1]
    for p in range(count):
        kpart[p] = kacc[p * rows : (p + 1) * rows]
    each_peer(lambda d: remote(kpart.at[ahead(d)], ksum.at[me], 4, d, ahead(d)).start())

    def take2(d):
        src = behind(d)
        remote(wgt.at[src], pen2.at[src], 2, d, src).wait_recv()
        gain([pen2[src, j] for j in range(xl)], src)

    each_peer(take2)
    channel_mix(wmt)

    def give2(d):
        peer = ahead(d)
        expand(stage2, peer)
        remote(stage2.at[peer], spec2.at[me], 3, d, peer).start()

    each_peer(give2)
    expand(stage2, me)
    ksum[me] = kpart[me]
    each_peer(lambda d: remote(kpart.at[0], ksum.at[behind(d)], 4, d, behind(d)).wait_recv())
    total = ksum[0]
    for p in range(1, count):
        total = total + ksum[p]
    kall[me] = total * (float(count * xl * ny * nz) ** -0.5)
    each_peer(lambda d: remote(kall.at[me], kall.at[me], 5, d, ahead(d)).start())

    mix(wb)

    def finish(y, planes):
        for x in range(xl):
            total = local[y, :, x * nz : (x + 1) * nz] + planes[x].astype(f32)
            out[x, y] = total.astype(bf16)

    finish(me, [stage2[me, j] for j in range(xl)])

    def last(d):
        src = behind(d)
        remote(stage2.at[src], spec2.at[src], 3, d, src).wait_recv()
        finish(src, [spec2[src, j] for j in range(xl)])

    each_peer(last)
    each_peer(lambda d: remote(kall.at[me], kall.at[behind(d)], 5, d, behind(d)).wait_recv())
    kout[...] = kall[...]

    def drain(d):
        peer = ahead(d)
        remote(feat.at[:, peer], pen1.at[me], 0, d, peer).wait_send()
        remote(stage1.at[peer], spec1.at[me], 1, d, peer).wait_send()
        remote(wgt.at[peer], pen2.at[me], 2, d, peer).wait_send()
        remote(stage2.at[peer], spec2.at[me], 3, d, peer).wait_send()
        remote(kpart.at[peer], ksum.at[me], 4, d, peer).wait_send()
        remote(kall.at[me], kall.at[me], 5, d, peer).wait_send()

    each_peer(drain)


def fits_kernel(count, features, kernel_weight):
    xl, ny, ch, nz = features.shape
    cells = xl * ny * ch * nz
    tile_rows = kernel_weight.shape[0] * ch
    if ny != count or nz % 128 or ch % 16 or tile_rows % (8 * count):
        return False
    return 80 * cells < 24 * 2**20


def fused_device(
    features,
    cotangent,
    wall_flags,
    mode_counts,
    offsets,
    point_weight,
    kernel_weight,
    lap_weight,
    spec_weight,
    bias,
):
    count = lax.axis_size("gx")
    if not fits_kernel(count, features, kernel_weight):
        return per_device(
            features,
            cotangent,
            wall_flags,
            mode_counts,
            offsets,
            point_weight,
            kernel_weight,
            lap_weight,
            spec_weight,
            bias,
        )
    xl, ny, ch, nz = features.shape
    modes, tiles = spec_weight.shape[0], kernel_weight.shape[0]
    kept = jnp.arange(modes, dtype=jnp.int32)[:, None] < mode_counts[None, :]
    masked = jnp.where(kept[:, :, None], spec_weight, jnp.zeros_like(spec_weight))
    stacked = jnp.concatenate([point_weight[None], lap_weight[None], kernel_weight], axis=0)
    forward = jnp.transpose(stacked, (1, 0, 2)).reshape(ch, (2 + tiles) * ch)
    backward = jnp.transpose(stacked, (2, 0, 1)).reshape(ch, (2 + tiles) * ch)
    rows = tiles * ch // count
    f32, bf16 = jnp.float32, jnp.bfloat16
    vmem = pl.BlockSpec(memory_space=pltpu.VMEM)
    smem = pl.BlockSpec(memory_space=pltpu.SMEM)
    field_grad, tile_grad = pl.pallas_call(
        functools.partial(fused_kernel, count),
        out_shape=(
            jax.ShapeDtypeStruct(features.shape, bf16),
            jax.ShapeDtypeStruct((count, rows, ch), f32),
        ),
        in_specs=[vmem, vmem, vmem, smem, smem, vmem, vmem, vmem, vmem, vmem],
        out_specs=(vmem, vmem),
        scratch_shapes=[
            pltpu.VMEM((2 * RAD + 1, xl + 2, ny + 2 * RAD, ch, nz), bf16),
            pltpu.VMEM((ny, (2 + tiles) * ch, xl * nz), bf16),
            pltpu.VMEM((ny, ch, xl * nz), f32),
            pltpu.VMEM((modes, ch, nz), f32),
            pltpu.VMEM((modes, ch, nz), f32),
            pltpu.VMEM((count, xl, ch, nz), bf16),
            pltpu.VMEM((count, xl, ch, nz), bf16),
            pltpu.VMEM((count, xl, ch, nz), bf16),
            pltpu.VMEM((count, xl, ch, nz), bf16),
            pltpu.VMEM((count, xl, ch, nz), bf16),
            pltpu.VMEM((count, xl, ch, nz), bf16),
            pltpu.VMEM((ny, xl, ch, nz), bf16),
            pltpu.VMEM((2, ny, ch, nz), bf16),
            pltpu.VMEM((2, ny, ch, nz), bf16),
            pltpu.VMEM((tiles * ch, ch), f32),
            pltpu.VMEM((count, rows, ch), f32),
            pltpu.VMEM((count, rows, ch), f32),
            pltpu.VMEM((count, rows, ch), f32),
            pltpu.VMEM((nz, 2 * RAD * nz), bf16),
            pltpu.SemaphoreType.DMA((6, count)),
            pltpu.SemaphoreType.DMA((6, count)),
            pltpu.SemaphoreType.DMA((4,)),
            pltpu.SemaphoreType.DMA((4,)),
        ],
        compiler_params=pltpu.CompilerParams(
            collective_id=0, has_side_effects=True, vmem_limit_bytes=48 * 2**20
        ),
    )(
        features,
        cotangent,
        wall_flags,
        offsets,
        basis_table(modes, count * xl).astype(f32),
        forward,
        backward,
        masked,
        jnp.swapaxes(masked, 1, 2),
        jnp.broadcast_to(bias[:, None], (ch, nz)),
    )
    return field_grad, tile_grad.reshape(kernel_weight.shape)


def solution(mesh):
    return jax.shard_map(
        fused_device,
        mesh=mesh,
        in_specs=(
            P(("groups", "gx"), None, None, None),
            P(("groups", "gx"), None, None, None),
            P(("groups", "gx"), None, None),
            P(),
            P(),
            P(),
            P(),
            P(),
            P(),
            P(),
        ),
        out_specs=(P(("groups", "gx"), None, None, None), P("groups", None, None)),
        check_vma=False,
    )
```
